32 devices in a mesh: dp: 8 (over z, x), seq: 4 (over y, core).
Axes of the slice: x: 2, y: 2, z: 4, core: 2. Of those that a mesh axis runs over, the one named last changes fastest.
Arguments:
- queries: bfloat16 [8, 512, 32, 128], P('dp', 'seq'), may hold values from -13 to 13
- keys: bfloat16 [8, 512, 4, 128], P('dp', 'seq'), may hold values from -13 to 13
- values: bfloat16 [8, 512, 4, 128], P('dp', 'seq'), may hold values from -6 to 6
- d_out: bfloat16 [8, 512, 32, 128], P('dp', 'seq'), may hold values from -6 to 6
- doc_ids: int32 [8, 512], P('dp', 'seq'), may hold values from 0 to 3, never falling along the last dimension, each value on 1 to 256 neighbouring positions
Outputs:
- query_grad: bfloat16 [8, 512, 32, 128], P('dp', 'seq')
- key_grad: bfloat16 [8, 512, 4, 128], P('dp', 'seq')
- value_grad: bfloat16 [8, 512, 4, 128], P('dp', 'seq')
- value_bias_grad: float32 [512], P('dp')
The draws below stay inside these ranges and needn't reach their ends.
Inputs may be any that keep to these rules, and one draw needn't show every extreme that they name: `doc_ids`: in each row the ids never fall along the tokens; each of the 4 ids marks one document of 1 to 256 tokens, and one document has exactly 256.
All inputs are finite; a program needn't handle non-finite values.
Results may differ from the reference program's by a relative error of at most 0.0073.
Values may be sent and summed in bfloat16 or wider, within the bound.
No kernel may reach another device: no remote copies, remote signals or barrier semaphores. Data moves between devices by JAX's collectives and lax.ppermute only.
A program may use at most 64 MiB of HBM per device.

```python
import math
import jax
import jax.numpy as jnp
import numpy as np
from jax import lax

QUERY_HEADS = 32
KEY_VALUE_HEADS = 4
HEAD_SIZE = 128
DOCS = 4
ROW_TOKENS = 512
MOST_LEN = 256
PACKED_ROWS = 8
TOKEN_TOTAL = 4096
N_SEQ = 4


def uncopied_heads(key, fold_tag, head_count):
    sampled_values = jax.random.normal(jax.random.fold_in(key, fold_tag), (PACKED_ROWS, ROW_TOKENS, head_count, HEAD_SIZE), jnp.float32)
    return jnp.clip(sampled_values, -6.0, 6.0)


def draw_queries(key, part):
    sampled_values = uncopied_heads(key, 1, QUERY_HEADS)
    return sampled_values.astype(jnp.bfloat16)


def draw_keys(key, part):
    sampled_values = uncopied_heads(key, 2, KEY_VALUE_HEADS)
    return sampled_values.astype(jnp.bfloat16)


def steps_of(own_key, extent, pieces, low, top_value):
    gain = 1.0
    for axis_at, shards_of in pieces:
        draws = jax.random.uniform(jax.random.fold_in(jax.random.fold_in(own_key, 6), axis_at), (shards_of,), jnp.float32, low / len(pieces), top_value / len(pieces))
        gain = gain * jnp.repeat(jnp.exp(draws), extent[axis_at] // shards_of).reshape((-1,) + (1,) * (len(extent) - 1 - axis_at))
    return gain


def profile(amount, total, most, lean):
    loads = [(1 << 20) // math.isqrt(grade ** lean) + 1 for grade in range(2, amount + 1)]
    surplus, given = total - most - (amount - 1), [1] * (amount - 1)
    while surplus > 0:
        movable = [i for i in range(amount - 1) if given[i] < most]
        mass, left = sum([loads[i] for i in movable]), surplus
        for i in movable:
            addition = min(most - given[i], max(1, left * loads[i] // mass), surplus)
            given[i] = given[i] + addition
            surplus = surplus - addition
    return np.array([most] + given)


def ragged_sizes(key, number_of, total, most, skew):
    if number_of == 2:
        one = jax.random.randint(key, (), max(1, total - most), min(most, total - 1) + 1)
        return jnp.stack([one, total - one])
    tallies = jnp.asarray(profile(number_of, total, most, skew), jnp.int32)
    twos = (number_of - 1) // 2
    source_of, receiver = tallies[1:1 + 2 * twos:2], tallies[2:2 + 2 * twos:2]
    margin = jnp.minimum(source_of - 1, most - receiver)
    passed = jax.random.randint(jax.random.fold_in(key, 1), (twos,), 0, 1 << 20) % (margin + 1)
    tallies = tallies.at[1:1 + 2 * twos:2].set(source_of - passed).at[2:2 + 2 * twos:2].set(receiver + passed)
    return tallies[jax.random.permutation(jax.random.fold_in(key, 2), number_of)]


def bell_draw(stream_key, shape, spread, bound, cuts=(), held_as=jnp.bfloat16):
    gain = steps_of(stream_key, shape, cuts, -0.22, 0.18) if cuts else 1.0
    values = jax.random.normal(stream_key, shape, jnp.float32) * spread * gain
    return jnp.minimum(jnp.maximum(values, -bound), bound).astype(held_as)


def setup_inputs(seed: int = 0) -> dict:
    seeds = jax.random.split(jax.random.key(seed), 6)
    queries = draw_queries(jax.random.fold_in(seeds[5], 71), 0)
    keys = draw_keys(jax.random.fold_in(seeds[5], 71), 0)
    values = bell_draw(seeds[2], (PACKED_ROWS, ROW_TOKENS, KEY_VALUE_HEADS, HEAD_SIZE), 1.0, 6.0, ((0, 8), (1, 4)))
    d_out = bell_draw(seeds[3], (PACKED_ROWS, ROW_TOKENS, QUERY_HEADS, HEAD_SIZE), 1.0, 6.0, ((0, 8), (1, 4)))
    doc_ids = jax.vmap(lambda own: jnp.searchsorted(jnp.cumsum(ragged_sizes(own, DOCS, ROW_TOKENS, MOST_LEN, 2)), jnp.arange(ROW_TOKENS), side="right"))(jax.random.split(seeds[4], PACKED_ROWS)).reshape((PACKED_ROWS, ROW_TOKENS)).astype(jnp.int32)
    return dict(queries=queries, keys=keys, values=values, d_out=d_out, doc_ids=doc_ids)


def copy_grads(queries, keys, values, d_out, allowed, copy_index):
    per_copy = QUERY_HEADS // N_SEQ
    head_copies = N_SEQ // KEY_VALUE_HEADS
    kv_group = copy_index // head_copies
    first_head = (copy_index * per_copy).astype(jnp.int32)
    q_heads = lax.dynamic_slice_in_dim(queries, first_head, per_copy, 1).astype(jnp.float32)
    o_heads = lax.dynamic_slice_in_dim(d_out, first_head, per_copy, 1).astype(jnp.float32)
    key_head = lax.dynamic_index_in_dim(keys, kv_group.astype(jnp.int32), 1, keepdims=False).astype(jnp.float32)
    value_head = lax.dynamic_index_in_dim(values, kv_group.astype(jnp.int32), 1, keepdims=False).astype(jnp.float32)
    score_scale = 1.0 / math.sqrt(HEAD_SIZE)
    scores = jnp.einsum('qhd,kd->hqk', q_heads, key_head) * score_scale
    masked = jnp.where(allowed[None], scores, -1e+30)
    row_top = lax.optimization_barrier(jnp.max(masked, axis=2, keepdims=True))
    exponent = jnp.where(allowed[None], jnp.exp(masked - row_top), 0.0)
    weights = exponent / lax.optimization_barrier(jnp.sum(exponent, axis=2, keepdims=True))
    dweights = jnp.einsum('qhd,kd->hqk', o_heads, value_head)
    row_delta = lax.optimization_barrier(jnp.sum(weights * dweights, axis=2, keepdims=True))
    dscores = weights * (dweights - row_delta)
    weights_b = lax.optimization_barrier(weights.astype(jnp.bfloat16)).astype(jnp.float32)
    dscores_b = lax.optimization_barrier(dscores.astype(jnp.bfloat16)).astype(jnp.float32)
    q_grad = (jnp.einsum('hqk,kd->qhd', dscores_b, key_head) * score_scale).astype(jnp.bfloat16)
    k_grad = (jnp.einsum('hqk,qhd->kd', dscores_b, q_heads) * score_scale).astype(jnp.bfloat16)
    v_grad = jnp.einsum('hqk,qhd->kd', weights_b, o_heads).astype(jnp.bfloat16)
    return (q_grad, k_grad, v_grad)

def row_grads(row_args):
    queries, keys, values, d_out, documents_per_row = row_args
    head_copies = N_SEQ // KEY_VALUE_HEADS
    position = jnp.arange(ROW_TOKENS, dtype=jnp.int32)
    allowed = (position[None, :] <= position[:, None]) & (documents_per_row[None, :] == documents_per_row[:, None])
    q_parts, key_pieces, value_pieces = lax.map(lambda copy_index: copy_grads(queries, keys, values, d_out, allowed, copy_index), jnp.arange(N_SEQ, dtype=jnp.int32))
    q_grad = jnp.transpose(q_parts, (1, 0, 2, 3)).reshape(ROW_TOKENS, QUERY_HEADS, HEAD_SIZE)
    summed_key = lax.optimization_barrier(jnp.sum(key_pieces.reshape(KEY_VALUE_HEADS, head_copies, ROW_TOKENS, HEAD_SIZE).astype(jnp.float32), axis=1))
    summed_value = lax.optimization_barrier(jnp.sum(value_pieces.reshape(KEY_VALUE_HEADS, head_copies, ROW_TOKENS, HEAD_SIZE).astype(jnp.float32), axis=1))
    k_grad = jnp.transpose(summed_key, (1, 0, 2)).astype(jnp.bfloat16)
    v_grad = jnp.transpose(summed_value, (1, 0, 2)).astype(jnp.bfloat16)
    return (q_grad, k_grad, v_grad, lax.optimization_barrier(jnp.sum(summed_value, axis=1)))

def reference(queries, keys, values, d_out, doc_ids):
    q_grad, k_grad, v_grad, row_bias = lax.map(row_grads, (queries, keys, values, d_out, doc_ids))
    total_bias = lax.optimization_barrier(jnp.sum(row_bias, axis=0)).reshape(KEY_VALUE_HEADS * HEAD_SIZE) / math.sqrt(TOKEN_TOTAL)
    return (q_grad, k_grad, v_grad, total_bias)
```

```python
import functools
import math

import jax
import jax.numpy as jnp
from jax import lax
from jax.experimental import pallas as pl
from jax.experimental.pallas import tpu as pltpu
from jax.sharding import PartitionSpec as P

masked_score = -1e30
rows_of_tile = 8


def dot(left, right, left_axis, right_axis):
    return lax.dot_general(
        left, right, (((left_axis,), (right_axis,)), ((), ())), preferred_element_type=jnp.float32
    )


def pick_head(head, tokens, heads):
    row = lax.broadcasted_iota(jnp.int32, (tokens, tokens * heads), 0)
    column = lax.broadcasted_iota(jnp.int32, (tokens, tokens * heads), 1)
    return (column == row * heads + head).astype(jnp.bfloat16)


def attention_kernel(near_count, score_scale, *refs):
    (place_ref, own_docs, near_docs, far_docs, queries, grads, key_refs, value_refs) = (
        refs[0],
        refs[1],
        refs[2 : 2 + near_count],
        refs[2 + near_count],
        refs[3 + near_count],
        refs[4 + near_count],
        refs[5 + near_count : 7 + 2 * near_count],
        refs[7 + 2 * near_count : 9 + 3 * near_count],
    )
    rest = refs[9 + 3 * near_count :]
    query_out, key_out, value_out, key_rows, value_rows, bias = rest
    group = pl.program_id(0)
    tokens, group_heads, head_dim = queries.shape
    chunks = near_count + 2
    heads = key_rows.shape[0]
    block = max(tokens // 4, 16)
    blocks = tokens // block
    rows = block * group_heads
    span = (near_count + 1) * tokens + block

    @pl.when(group == 0)
    def _():
        place = place_ref[0]
        for head in range(heads):
            chosen = pick_head(head, tokens, heads)
            for at in range(chunks):
                into = pl.ds(at * tokens, tokens)
                key_rows[head, into, :] = dot(chosen, key_refs[at][...], 1, 0).astype(jnp.bfloat16)
                value_rows[head, into, :] = dot(chosen, value_refs[at][...], 1, 0).astype(
                    jnp.bfloat16
                )
        own = own_docs[...]
        all_docs = jnp.concatenate([far_docs[...]] + [d[...] for d in near_docs] + [own], axis=1)
        key_ids = jnp.transpose(
            jnp.broadcast_to(all_docs.astype(jnp.float32), (rows_of_tile, chunks * tokens))
        )[:, :1]
        own_ids = jnp.broadcast_to(own.astype(jnp.float32), (rows_of_tile, tokens)).astype(
            jnp.bfloat16
        )
        for at in range(blocks):
            token = lax.broadcasted_iota(jnp.int32, (tokens, rows), 0)
            lane = lax.broadcasted_iota(jnp.int32, (tokens, rows), 1)
            spread = (token == at * block + lane // group_heads).astype(jnp.bfloat16)
            query_ids = dot(own_ids, spread, 1, 0)[:1]
            key_place = at * block + lax.broadcasted_iota(jnp.int32, (span, rows), 0)
            query_place = (
                (chunks - 1) * tokens
                + at * block
                + lax.broadcasted_iota(jnp.int32, (span, rows), 1) // group_heads
            )
            allowed = (
                (key_place <= query_place)
                & (key_place >= (chunks - 1 - place) * tokens)
                & (key_ids[at * block : at * block + span] == query_ids)
            )
            bias[at] = jnp.where(allowed, 0.0, masked_score)

    key_out[...] = jnp.zeros_like(key_out)
    value_out[...] = jnp.zeros_like(value_out)
    for at in range(blocks):
        some = slice(at * block, (at + 1) * block)
        keys_at = pl.ds(at * block, span)
        query = queries[some].reshape(rows, head_dim)
        grad = grads[some].reshape(rows, head_dim)
        key = key_rows[group, keys_at, :]
        value = value_rows[group, keys_at, :]
        scores = dot(key, query, 1, 1) * (score_scale * math.log2(math.e)) + bias[at]
        exponent = jnp.exp2(scores - jnp.max(scores, axis=0, keepdims=True))
        weights = exponent * (1.0 / jnp.sum(exponent, axis=0, keepdims=True))
        dweights = dot(value, grad, 1, 1)
        row_delta = jnp.sum(weights * dweights, axis=0, keepdims=True)
        dscores = (weights * (dweights - row_delta)).astype(jnp.bfloat16)
        value_out[0, keys_at, :] += dot(weights.astype(jnp.bfloat16), grad, 1, 0)
        key_out[0, keys_at, :] += dot(dscores, query, 1, 0)
        query_grad = dot(dscores, key, 0, 0) * score_scale
        query_out[some] = query_grad.astype(jnp.bfloat16).reshape(block, group_heads, head_dim)
    key_out[...] = key_out[...] * score_scale


def attention(place, docs, queries, grads, keys, values, kv_heads, score_scale):
    tokens, heads, head_dim = queries.shape
    chunks = len(keys)
    near = chunks - 2
    group_heads = heads // kv_heads
    block = max(tokens // 4, 16)
    span = (near + 1) * tokens + block
    head_block = pl.BlockSpec((tokens, group_heads, head_dim), lambda g: (0, g, 0))
    sum_block = pl.BlockSpec((1, chunks * tokens, head_dim), lambda g: (g, 0, 0))
    vmem = pl.BlockSpec(memory_space=pltpu.VMEM)
    sums = jax.ShapeDtypeStruct((kv_heads, chunks * tokens, head_dim), jnp.float32)
    return pl.pallas_call(
        functools.partial(attention_kernel, near, score_scale),
        out_shape=(jax.ShapeDtypeStruct(queries.shape, jnp.bfloat16), sums, sums),
        grid=(kv_heads,),
        in_specs=[pl.BlockSpec(memory_space=pltpu.SMEM)]
        + [vmem] * chunks
        + [head_block, head_block]
        + [vmem] * (2 * chunks),
        out_specs=(head_block, sum_block, sum_block),
        scratch_shapes=[
            pltpu.VMEM((kv_heads, chunks * tokens, head_dim), jnp.bfloat16),
            pltpu.VMEM((kv_heads, chunks * tokens, head_dim), jnp.bfloat16),
            pltpu.VMEM((tokens // block, span, block * group_heads), jnp.float32),
        ],
        name="attention",
    )(place, docs[-1], *docs[1:-1], docs[0], queries, grads, *keys, *values)


def finish_kernel(kv_heads, *refs):
    own_key, own_value, key_more, value_more, key_out, value_out = refs
    tokens = own_key.shape[1]
    for own, more, out in ((own_key, key_more, key_out), (own_value, value_more, value_out)):
        total = None
        for head in range(kv_heads):
            half = (own[head] + more[head].astype(jnp.float32)).astype(jnp.bfloat16)
            placed = dot(pick_head(head, tokens, kv_heads), half, 0, 0)
            total = placed if total is None else total + placed
        out[...] = total.astype(jnp.bfloat16)


def shards(queries, keys, values, d_out, doc_ids):
    seq_size = lax.axis_size("seq")
    place = lax.axis_index("seq")
    tokens, kv_heads, head_dim = keys.shape[1:]
    heads = queries.shape[2]
    halo = seq_size // 2
    score_scale = 1.0 / math.sqrt(head_dim)
    key_local = keys.reshape(tokens * kv_heads, head_dim)
    value_local = values.reshape(tokens * kv_heads, head_dim)

    def swap(array, distance):
        pairs = [(i, i ^ distance) for i in range(seq_size)]
        return lax.ppermute(array, "seq", pairs)

    def shift(array, distance):
        pairs = [(i, (i + distance) % seq_size) for i in range(seq_size)]
        return lax.ppermute(array, "seq", pairs)

    odd = place % 2 == 1
    if halo == 2:
        def fetch(array):
            beside, far = swap(array, 1), swap(array, 2)
            return (far, jnp.where(odd, beside, swap(far, 1)), array)
    else:
        def fetch(array):
            return tuple(shift(array, d) for d in range(halo, 0, -1)) + (array,)

    docs, key_all, value_all = fetch(doc_ids), fetch(key_local), fetch(value_local)
    query_grad, key_sums, value_sums = attention(
        place.reshape(1), docs, queries[0], d_out[0], key_all, value_all, kv_heads, score_scale
    )

    def part(array, at):
        return array[:, at * tokens : (at + 1) * tokens]

    def give_back(sums):
        own, far = part(sums, halo), part(sums, 0)
        if halo == 2:
            got = swap(part(sums, 1).astype(jnp.bfloat16), 1).astype(jnp.float32)
            got_far = jnp.where(odd, got, 0.0)
            own = own + jnp.where(odd, 0.0, got)
            more = swap((far + got_far).astype(jnp.bfloat16), 2)
            return (own, more)
        more = 0.0
        for at in range(halo):
            back = shift(part(sums, at).astype(jnp.bfloat16), at - halo).astype(jnp.float32)
            more = more + jnp.where(place < seq_size - halo + at, back, 0.0)
        return (own, more)

    own_value, value_more = give_back(value_sums)
    own_key, key_more = give_back(key_sums)
    flat = jax.ShapeDtypeStruct((tokens * kv_heads, head_dim), jnp.bfloat16)
    key_grad, value_grad = pl.pallas_call(
        functools.partial(finish_kernel, kv_heads), out_shape=(flat, flat), name="finish"
    )(own_key, own_value, key_more, value_more)

    bias = jnp.sum(
        d_out[0].astype(jnp.float32).reshape(tokens, kv_heads, heads // kv_heads, head_dim), (0, 2)
    )
    total_tokens = tokens * seq_size
    for axis in ("seq", "dp"):
        size = lax.axis_size(axis)
        step = 1
        while step < size:
            bias = bias + lax.ppermute(bias, axis, [(i, i ^ step) for i in range(size)])
            step *= 2
    dp_size = lax.axis_size("dp")
    total_tokens = total_tokens * dp_size
    width = kv_heads * head_dim // dp_size
    bias = lax.dynamic_slice_in_dim(bias.reshape(-1), lax.axis_index("dp") * width, width)
    return (
        query_grad[None],
        key_grad.reshape(keys.shape),
        value_grad.reshape(values.shape),
        bias / math.sqrt(total_tokens),
    )


def solution(mesh):
    placed = P("dp", "seq", None, None)
    return jax.shard_map(
        shards,
        mesh=mesh,
        in_specs=(placed, placed, placed, placed, P("dp", "seq")),
        out_specs=(placed, placed, placed, P("dp")),
        check_vma=False,
    )
```
